32 devices in a mesh: row: 4 (over y, x), col: 8 (over z, core).
Axes of the slice: x: 2, y: 2, z: 4, core: 2. Of those that a mesh axis runs over, the one named last changes fastest.
Arguments:
- transmission: float32 [2, 2, 512, 1024], P(None, None, 'row', 'col'), may hold values from -6 to 6
- probe: float32 [2, 256, 256], replicated, may hold values from -6 to 6
- fresnel_phase: float32 [256, 256], replicated, may hold values from -3.140625 to 3.140625
- amplitudes: float32 [4, 8, 1, 256, 256], P('row', 'col'), may hold values from 0.3 to 4
- positions: int32 [4, 8, 1, 2], P('row', 'col'), may hold values from 0 to 72, as said below
- tv_weight: float32 [512, 1024], P('row', 'col'), may hold values from 0.3 to 3
Outputs:
- refined: float32 [2, 2, 512, 1024], P(None, None, 'row', 'col')
The draws below stay inside these ranges and needn't reach their ends.
Inputs may be any that keep to these rules, and one draw needn't show every extreme that they name: `positions`: over all tiles and views together, for each of the two coordinates, some view has offset 0 and some view has offset 2 * 36; a view covers rows and columns [offset, offset + 256) of its tile's region.
All inputs are finite; a program needn't handle non-finite values.
Results may differ from the reference program's by a relative error of at most 0.00016.
Values sent between devices are 32-bit elements; how exact they have to be, the bound alone decides.
A program may use at most 64 MiB of HBM per device.

```python
import math
import jax
import jax.numpy as jnp
from jax import lax

CORE = 128
PROBE = 256
SHIFT = 36
VIEWS = 1
SLICES = 2
TV_STEPS = 3
HALO = 100
EXTENT = 328
ROWS_ALL = 512
COLS_ALL = 1024
N_ROW = 4
N_COL = 8


def draw_positions(key, part):
    value_key, score_key = jax.random.split(key)
    entries = N_ROW * N_COL * VIEWS
    values = jax.random.randint(value_key, (entries, 2), 0, 2 * SHIFT + 1, dtype=jnp.int32)
    entry_index = jnp.arange(entries, dtype=jnp.int32)
    scores = jax.random.randint(score_key, (entries, 2), 0, 1 << 12, dtype=jnp.int32)
    scores = scores * entries + entry_index[:, None]
    ordering = jnp.argsort(scores, axis=0, stable=True)
    ranking = jnp.argsort(ordering, axis=0, stable=True)
    lowest = jnp.zeros_like(values)
    highest = jnp.full_like(values, 2 * SHIFT)
    chosen = jnp.where(ranking == 0, lowest, jnp.where(ranking == 1, highest, values))
    return chosen.reshape(N_ROW, N_COL, VIEWS, 2).astype(jnp.int32)


def levels(rng, dims, cuts, smallest, high):
    level = 1.0
    for position, shards_of in cuts:
        heights = jax.random.uniform(jax.random.fold_in(jax.random.fold_in(rng, 6), position), (shards_of,), jnp.float32, smallest / len(cuts), high / len(cuts))
        level = level * jnp.repeat(jnp.exp(heights), dims[position] // shards_of).reshape((-1,) + (1,) * (len(dims) - 1 - position))
    return level


def bell_draw(stream_key, shape, scale, limit, cuts=(), kind=jnp.bfloat16):
    gain = levels(stream_key, shape, cuts, -0.22, 0.18) if cuts else 1.0
    values = jax.random.normal(stream_key, shape, jnp.float32) * scale * gain
    return jnp.minimum(jnp.maximum(values, -limit), limit).astype(kind)


def setup_inputs(seed: int = 0) -> dict:
    keys = jax.random.split(jax.random.key(seed), 7)
    transmission = bell_draw(keys[0], (SLICES, 2, ROWS_ALL, COLS_ALL), 1.0, 6.0, ((2, 4), (3, 8)), jnp.float32)
    probe = bell_draw(keys[1], (2, PROBE, PROBE), 1.0, 6.0, (), jnp.float32)
    fresnel_phase = jnp.clip(jax.random.uniform(keys[2], (PROBE, PROBE), jnp.float32, -3.140625, 3.140625), -3.140625, 3.140625)
    amplitudes = jnp.clip(jnp.exp(math.log(4.0) - 2.5902671 * jax.random.uniform(keys[3], (N_ROW, N_COL, VIEWS, PROBE, PROBE), jnp.float32) ** levels(keys[3], (N_ROW, N_COL, VIEWS, PROBE, PROBE), ((0, 4), (1, 8)), -0.2, 0.2)), 0.3, 4.0)
    positions = draw_positions(jax.random.fold_in(keys[6], 71), 0)
    tv_weight = jnp.clip(jnp.exp(math.log(3.0) - 2.3025851 * jax.random.uniform(keys[5], (ROWS_ALL, COLS_ALL), jnp.float32) ** levels(keys[5], (ROWS_ALL, COLS_ALL), ((0, 4), (1, 8)), -0.2, 0.2)), 0.3, 3.0)
    return {"transmission": transmission, "probe": probe, "fresnel_phase": fresnel_phase, "amplitudes": amplitudes, "positions": positions, "tv_weight": tv_weight}


AMP_EPS = 0.1
LEARN_RATE = 0.2
TV_EPS = 1.0
TV_TAU = 0.1

def forward_two(field):
    return jnp.fft.fft2(field, norm='ortho')

def inverse_two(field):
    return jnp.fft.ifft2(field, norm='ortho')

def view_gradient(extended, probe_wave, kernel, measured, offset):
    anchor = jnp.zeros((), jnp.int32)
    windows = []
    for s in range(SLICES):
        window = lax.dynamic_slice(extended[s], (anchor, offset[0], offset[1]), (2, PROBE, PROBE))
        windows.append(window[0] + 1j * window[1])
    wave = probe_wave
    incoming = []
    for s in range(SLICES):
        incoming.append(wave)
        exit_wave = windows[s] * wave
        if s < SLICES - 1:
            wave = inverse_two(kernel * forward_two(exit_wave))
    far_field = forward_two(exit_wave)
    magnitude = jnp.sqrt(jnp.real(far_field) ** 2 + jnp.imag(far_field) ** 2 + AMP_EPS)
    adjoint = inverse_two(far_field * (1.0 - measured / magnitude))
    gradients = []
    for s in range(SLICES - 1, -1, -1):
        single = jnp.conj(incoming[s]) * adjoint
        gradients.insert(0, jnp.stack([jnp.real(single), jnp.imag(single)]))
        if s > 0:
            adjoint = inverse_two(jnp.conj(kernel) * forward_two(jnp.conj(windows[s]) * adjoint))
    return jnp.stack(gradients)

def tv_step(field, weight):
    padded = jnp.pad(field, ((0, 0), (0, 0), (0, 1), (0, 1)))
    down_diff = padded[:, :, 1:, :-1] - field
    right_diff = padded[:, :, :-1, 1:] - field
    spread = jnp.sqrt(lax.optimization_barrier(jnp.sum(down_diff * down_diff + right_diff * right_diff, axis=1, keepdims=True)) + TV_EPS)
    down_flux = weight * down_diff / spread
    right_flux = weight * right_diff / spread
    down_prev = jnp.pad(down_flux, ((0, 0), (0, 0), (1, 0), (0, 0)))[:, :, :-1, :]
    right_prev = jnp.pad(right_flux, ((0, 0), (0, 0), (0, 0), (1, 0)))[:, :, :, :-1]
    return field + TV_TAU * (down_flux - down_prev + right_flux - right_prev)

def reference(transmission, probe, fresnel_phase, amplitudes, positions, tv_weight):
    probe_wave = probe[0] + 1j * probe[1]
    kernel = jnp.cos(fresnel_phase) + 1j * jnp.sin(fresnel_phase)
    padded = jnp.pad(transmission, ((0, 0), (0, 0), (HALO, HALO), (HALO, HALO)))
    anchor = jnp.zeros((), jnp.int32)

    def add_tile(k, summed):
        tile_row = (k // N_COL).astype(jnp.int32)
        tile_col = (k % N_COL).astype(jnp.int32)
        corner = (anchor, anchor, tile_row * CORE, tile_col * CORE)
        extended = lax.dynamic_slice(padded, corner, (SLICES, 2, EXTENT, EXTENT))

        def add_view(v, local):
            view = jnp.asarray(v).astype(jnp.int32)
            offset = positions[tile_row, tile_col, view]
            gradient = view_gradient(extended, probe_wave, kernel, amplitudes[tile_row, tile_col, view], offset)
            place = (anchor, anchor, offset[0], offset[1])
            current = lax.dynamic_slice(local, place, (SLICES, 2, PROBE, PROBE))
            return lax.dynamic_update_slice(local, current + gradient, place)
        local = lax.fori_loop(0, VIEWS, add_view, jnp.zeros((SLICES, 2, EXTENT, EXTENT), jnp.float32))
        current = lax.dynamic_slice(summed, corner, (SLICES, 2, EXTENT, EXTENT))
        return lax.dynamic_update_slice(summed, current + local, corner)
    summed = lax.fori_loop(0, N_ROW * N_COL, add_tile, jnp.zeros(padded.shape, jnp.float32))
    gradient = summed[:, :, HALO:HALO + ROWS_ALL, HALO:HALO + COLS_ALL]
    field = transmission - LEARN_RATE * gradient
    for step in range(TV_STEPS):
        field = tv_step(field, tv_weight)
    return field
```

```python
import functools
import math

import jax
import jax.numpy as jnp
import numpy as np
from jax import lax
from jax.experimental import pallas as pl
from jax.experimental.pallas import tpu as pltpu
from jax.sharding import PartitionSpec as P

MESH = pl.DeviceIdType.MESH
F32, BF16 = jnp.float32, jnp.bfloat16
CORE = 128
PROBE = 256
HALF = 128
BAND = 104
ROWS = BAND + CORE + BAND
COLS = 3 * CORE
HALO = 100
REACH = 3
TVROWS = 136
UPROWS = 112
AMP_EPS = 0.1
LEARN_RATE = 0.2
TV_EPS = 1.0
TV_TAU = 0.1
TV_STEPS = 3


def tables():
    k, j = np.arange(HALF)[:, None], np.arange(HALF)[None, :]
    parts = []
    for odd in (0, 1):
        angle = 2.0 * np.pi * (((2 * k + odd) * j) % PROBE) / PROBE
        c, s = np.cos(angle) / math.sqrt(PROBE), np.sin(angle) / math.sqrt(PROBE)
        full = np.block([[c, s], [-s, c]])
        parts.append(full)
    out = []
    for full in (parts[0], parts[0].T, parts[1], parts[1].T):
        full = full.astype(np.float32)
        high = full.astype(BF16)
        out += [high, (full - high.astype(np.float32)).astype(BF16)]
    order = np.zeros((PROBE, PROBE), np.float32)
    order[np.arange(HALF), 2 * np.arange(HALF)] = 1
    order[HALF + np.arange(HALF), 2 * np.arange(HALF) + 1] = 1
    out += [order.astype(BF16), order.T.astype(BF16)]
    return np.stack(out)


def split(x):
    high = x.astype(BF16)
    return high, (x - high.astype(F32)).astype(BF16)


def mm(a, b):
    return jnp.dot(a, b, preferred_element_type=F32)


def left(tab, i, x):
    wh, wl = tab[2 * i], tab[2 * i + 1]
    xh, xl = split(x)
    return mm(wh, xh) + (mm(wh, xl) + mm(wl, xh))


def right(tab, i, x):
    wh, wl = tab[2 * i], tab[2 * i + 1]
    xh, xl = split(x)
    return mm(xh, wh) + (mm(xl, wh) + mm(xh, wl))


def cat(a, b, axis):
    return jnp.concatenate([a, b], axis=axis)


def forward(tab, re, im):
    h = HALF
    e = left(tab, 0, cat(re[:h] + re[h:], im[:h] + im[h:], 0))
    o = left(tab, 2, cat(re[:h] - re[h:], im[:h] - im[h:], 0))
    re, im = cat(e[:h], o[:h], 0), cat(e[h:], o[h:], 0)
    e = right(tab, 1, cat(re[:, :h] + re[:, h:], im[:, :h] + im[:, h:], 1))
    o = right(tab, 3, cat(re[:, :h] - re[:, h:], im[:, :h] - im[:, h:], 1))
    return cat(e[:, :h], o[:, :h], 1), cat(e[:, h:], o[:, h:], 1)


def inverse(tab, re, im):
    h = HALF
    e = left(tab, 1, cat(re[:h], im[:h], 0))
    o = left(tab, 3, cat(re[h:], im[h:], 0))
    s, d = e + o, e - o
    re, im = cat(s[:h], d[:h], 0), cat(s[h:], d[h:], 0)
    e = right(tab, 0, cat(re[:, :h], im[:, :h], 1))
    o = right(tab, 2, cat(re[:, h:], im[:, h:], 1))
    s, d = e + o, e - o
    return cat(s[:, :h], d[:, :h], 1), cat(s[:, h:], d[:, h:], 1)


def reorder(tab, x):
    for axis in (0, 1):
        total = None
        rest = x
        for _ in range(3):
            part = rest.astype(BF16)
            rest = rest - part.astype(F32)
            term = mm(tab[8], part) if axis == 0 else mm(part, tab[9])
            total = term if total is None else total + term
        x = total
    return x


class Place:
    def __init__(self):
        self.r, self.c = lax.axis_index("row"), lax.axis_index("col")
        nr, nc = lax.axis_size("row"), lax.axis_size("col")
        self.has = {"up": self.r > 0, "down": self.r < nr - 1, "left": self.c > 0, "right": self.c < nc - 1}
        self.to = {"up": {"row": self.r - 1}, "down": {"row": self.r + 1}, "left": {"col": self.c - 1}, "right": {"col": self.c + 1}}

    def barrier(self):
        sem = pltpu.get_barrier_semaphore()
        for side in OPPOSITE:
            @pl.when(self.has[side])
            def _():
                pl.semaphore_signal(sem, inc=1, device_id=self.to[side], device_id_type=MESH)
        pl.semaphore_wait(sem, sum(self.has[side].astype(jnp.int32) for side in OPPOSITE))


OPPOSITE = {"up": "down", "down": "up", "left": "right", "right": "left"}


class Copy:
    def __init__(self, place, side, src, dst, sems, i, also=None):
        self.op = pltpu.make_async_remote_copy(
            src_ref=src, dst_ref=dst, send_sem=sems[0].at[i], recv_sem=sems[1].at[i],
            device_id=place.to[side], device_id_type=MESH,
        )
        self.sends, self.gets = place.has[side], place.has[OPPOSITE[side]]
        if also is not None:
            self.sends, self.gets = self.sends & also, self.gets & also

    def start(self):
        pl.when(self.sends)(lambda: self.op.start())

    def got(self):
        pl.when(self.gets)(lambda: self.op.wait_recv())

    def sent(self):
        pl.when(self.sends)(lambda: self.op.wait_send())


def exchange_kernel(tr, w, ext, wext, send, recv):
    place = Place()
    has = place.has
    sems = (send, recv)
    place.barrier()
    mid = pl.ds(CORE, CORE)
    lanes = {"left": pl.ds(2 * CORE, CORE), "right": pl.ds(0, CORE)}
    jobs = []
    for ch in range(5):
        band = BAND if ch < 4 else 8
        src = tr.at[ch] if ch < 4 else w
        dst = ext.at[ch] if ch < 4 else wext
        jobs.append((band, src, dst))
    copies, corners = [], []
    for ch, (band, src, dst) in enumerate(jobs):
        base = 8 * ch
        top, low = pl.ds(0, band), pl.ds(band + CORE, band)
        group = [
            Copy(place, "up", src.at[pl.ds(0, band)], dst.at[low, mid], sems, base),
            Copy(place, "down", src.at[pl.ds(CORE - band, band)], dst.at[top, mid], sems, base + 1),
            Copy(place, "left", src, dst.at[pl.ds(band, CORE), lanes["left"]], sems, base + 2),
            Copy(place, "right", src, dst.at[pl.ds(band, CORE), lanes["right"]], sems, base + 3),
        ]
        for c in group:
            c.start()
        copies.append(group)
        corner = []
        for n, (rows, there) in enumerate(((low, has["down"]), (top, has["up"]))):
            for m, side in enumerate(("left", "right")):
                corner.append(Copy(place, side, dst.at[rows, mid], dst.at[rows, lanes[side]], sems, base + 4 + 2 * n + m, there))
        corners.append(corner)
    for (band, src, dst) in jobs:
        dst[band : band + CORE, CORE : 2 * CORE] = src[...]
        total = dst.shape[0]

        @pl.when(jnp.logical_not(has["up"]))
        def _():
            dst[0:band, :] = jnp.zeros((band, COLS), F32)

        @pl.when(jnp.logical_not(has["down"]))
        def _():
            dst[band + CORE : total, :] = jnp.zeros((band, COLS), F32)

        @pl.when(jnp.logical_not(has["left"]))
        def _():
            dst[:, 0:CORE] = jnp.zeros((total, CORE), F32)

        @pl.when(jnp.logical_not(has["right"]))
        def _():
            dst[:, 2 * CORE :] = jnp.zeros((total, CORE), F32)
    for ch in range(5):
        for n in (0, 1):
            copies[ch][n].got()
            for m in (0, 1):
                corners[ch][2 * n + m].start()
    for ch in range(5):
        for c in copies[ch][2:] + corners[ch]:
            c.got()
        for c in copies[ch] + corners[ch]:
            c.sent()


def view_kernel(pos, ext, probe, phase, amp, tab, own, lband):
    p, q = pos[0], pos[1]

    def window(ch):
        rows = pltpu.roll(ext[ch], ROWS - (BAND - HALO) - p, 0)[:PROBE]
        return pltpu.roll(rows, COLS - (q + (CORE - HALO)), 1)[:, :PROBE]

    def put(ch, grad):
        wide = cat(grad, jnp.zeros((PROBE, COLS - PROBE), F32), 1)
        wide = cat(wide, jnp.zeros((ROWS - PROBE, COLS), F32), 0)
        wide = pltpu.roll(wide, p + (BAND + REACH - HALO), 0)
        at_own = lax.rem(q + (COLS - HALO + REACH), COLS)
        own[ch] = pltpu.roll(wide, at_own, 1)[:, :PROBE]
        lband[ch] = pltpu.roll(wide, q + (CORE - REACH - HALO), 1)[:, :CORE]

    phase = reorder(tab, phase[...])
    kr, ki = jnp.cos(phase), jnp.sin(phase)
    measured = reorder(tab, amp[...])
    ar, ai = window(0), window(1)
    br, bi = window(2), window(3)
    pr, pi = probe[0], probe[1]
    fr, fi = forward(tab, ar * pr - ai * pi, ar * pi + ai * pr)
    wr, wi = inverse(tab, kr * fr - ki * fi, kr * fi + ki * fr)
    fr, fi = forward(tab, br * wr - bi * wi, br * wi + bi * wr)
    factor = 1.0 - measured / jnp.sqrt(fr * fr + fi * fi + AMP_EPS)
    gr, gi = inverse(tab, fr * factor, fi * factor)
    put(2, wr * gr + wi * gi)
    put(3, wr * gi - wi * gr)
    fr, fi = forward(tab, br * gr + bi * gi, br * gi - bi * gr)
    gr, gi = inverse(tab, kr * fr + ki * fi, kr * fi - ki * fr)
    put(0, pr * gr + pi * gi)
    put(1, pr * gi - pi * gr)


def fold_kernel(own, lband, ext, wext, out, from_left, from_right, total, from_up, from_down, send, recv):
    place = Place()
    has = place.has
    sems = (send, recv)
    place.barrier()
    order = (2, 3, 0, 1)
    across = {}
    for ch in order:
        across[ch] = (
            Copy(place, "right", own.at[ch, :, pl.ds(CORE, CORE)], from_left.at[ch], sems, 2 * ch),
            Copy(place, "left", lband.at[ch], from_right.at[ch], sems, 2 * ch + 1),
        )
        for c in across[ch]:
            c.start()

    for side, ref in (("left", from_left), ("right", from_right), ("up", from_up), ("down", from_down)):
        @pl.when(jnp.logical_not(has[side]))
        def _():
            ref[...] = jnp.zeros(ref.shape, F32)

    lane = lax.broadcasted_iota(jnp.int32, (ROWS, CORE), 1)
    packed = jnp.zeros((ROWS, CORE), F32)
    along = []
    for n, ch in enumerate(order + (4,)):
        if ch < 4:
            for c in across[ch]:
                c.got()
            shifted = pltpu.roll(from_right[ch], 2 * REACH, 1)
            total[ch] = own[ch, :, :CORE] + from_left[ch] + jnp.where(lane >= 2 * REACH, shifted, 0.0)
            rest = jnp.where(lane < 2 * REACH, own[ch, :, CORE:] + shifted, 0.0)
            packed = packed + (pltpu.roll(rest, 8 * ch, 1) if ch else rest)
        else:
            total[4] = packed
        pair = (
            Copy(place, "down", total.at[ch, pl.ds(ROWS - BAND, BAND)], from_up.at[ch], sems, 8 + 2 * ch),
            Copy(place, "up", total.at[ch, pl.ds(0, UPROWS)], from_down.at[ch], sems, 9 + 2 * ch),
        )
        for c in pair:
            c.start()
        along.append(pair)

    grad = {}
    for pair, ch in zip(along, order + (4,)):
        for c in pair:
            c.got()
        mine = total[ch, BAND : BAND + TVROWS, :]
        upper = cat(from_up[ch], jnp.zeros((TVROWS - BAND, CORE), F32), 0)
        lower = cat(jnp.zeros((TVROWS - UPROWS, CORE), F32), from_down[ch], 0)
        grad[ch] = mine + upper + lower

    shape = (TVROWS, PROBE)
    row_at = lax.broadcasted_iota(jnp.int32, shape, 0) - REACH + place.r * CORE
    col_at = lax.broadcasted_iota(jnp.int32, shape, 1) - REACH + place.c * CORE
    inside = (row_at >= 0) & (row_at < lax.axis_size("row") * CORE) & (col_at >= 0) & (col_at < lax.axis_size("col") * CORE)
    inside = inside.astype(F32)

    def cut(ref_rows):
        return pltpu.roll(ref_rows, COLS - (CORE - REACH), 1)[:, :PROBE]

    weight = cut(wext[8 - REACH : 8 - REACH + TVROWS, :]) * inside
    fields = []
    for ch in range(4):
        rest = pltpu.roll(grad[4], CORE - 8 * ch, 1) if ch else grad[4]
        field = cut(ext[ch, BAND - REACH : BAND - REACH + TVROWS, :])
        fields.append((field - LEARN_RATE * cat(grad[ch], rest, 1)) * inside)
    for s in range(2):
        pair = fields[2 * s : 2 * s + 2]
        for _ in range(TV_STEPS):
            down = [pltpu.roll(f, TVROWS - 1, 0) - f for f in pair]
            along_row = [pltpu.roll(f, PROBE - 1, 1) - f for f in pair]
            square = down[0] * down[0] + along_row[0] * along_row[0] + (down[1] * down[1] + along_row[1] * along_row[1])
            gain = weight / jnp.sqrt(square + TV_EPS)
            fresh = []
            for f, d, r in zip(pair, down, along_row):
                d, r = gain * d, gain * r
                update = d - pltpu.roll(d, 1, 0) + (r - pltpu.roll(r, 1, 1))
                fresh.append((f + TV_TAU * update) * inside)
            pair = fresh
        for c in range(2):
            out[2 * s + c] = pltpu.roll(pair[c], PROBE - REACH, 1)[REACH : REACH + CORE, :CORE]
    for ch in order:
        for c in across[ch]:
            c.sent()
    for pair in along:
        for c in pair:
            c.sent()


def spec():
    return pl.BlockSpec(memory_space=pltpu.VMEM)


def shape_of(*dims):
    return jax.ShapeDtypeStruct(dims, F32)


def body(transmission, probe, fresnel_phase, amplitudes, positions, tv_weight):
    tr = transmission.reshape(4, CORE, CORE)
    tab = jnp.asarray(tables())
    ext, wext = pl.pallas_call(
        exchange_kernel,
        out_shape=(shape_of(4, ROWS, COLS), shape_of(CORE + 16, COLS)),
        in_specs=[spec()] * 2,
        out_specs=(spec(), spec()),
        scratch_shapes=[pltpu.SemaphoreType.DMA((40,)), pltpu.SemaphoreType.DMA((40,))],
        compiler_params=pltpu.CompilerParams(collective_id=0, has_side_effects=True),
        name="exchange",
    )(tr, tv_weight)
    own, lband = pl.pallas_call(
        view_kernel,
        out_shape=(shape_of(4, ROWS, PROBE), shape_of(4, ROWS, CORE)),
        in_specs=[pl.BlockSpec(memory_space=pltpu.SMEM)] + [spec()] * 5,
        out_specs=(spec(), spec()),
        name="view",
    )(positions.reshape(2), ext, probe, fresnel_phase, amplitudes.reshape(PROBE, PROBE), tab)
    out = pl.pallas_call(
        fold_kernel,
        out_shape=shape_of(4, CORE, CORE),
        in_specs=[spec()] * 4,
        out_specs=spec(),
        scratch_shapes=[
            pltpu.VMEM((4, ROWS, CORE), F32),
            pltpu.VMEM((4, ROWS, CORE), F32),
            pltpu.VMEM((5, ROWS, CORE), F32),
            pltpu.VMEM((5, BAND, CORE), F32),
            pltpu.VMEM((5, UPROWS, CORE), F32),
            pltpu.SemaphoreType.DMA((18,)),
            pltpu.SemaphoreType.DMA((18,)),
        ],
        compiler_params=pltpu.CompilerParams(collective_id=1, has_side_effects=True),
        name="fold",
    )(own, lband, ext, wext)
    return out.reshape(2, 2, CORE, CORE)


def solution(mesh):
    placed = (
        P(None, None, "row", "col"),
        P(),
        P(),
        P("row", "col", None, None, None),
        P("row", "col", None, None),
        P("row", "col"),
    )
    return jax.shard_map(
        body, mesh=mesh, in_specs=placed, out_specs=P(None, None, "row", "col"), check_vma=False
    )
```

```python
import functools
import math

import jax
import jax.numpy as jnp
import numpy as np
from jax import lax
from jax.experimental import pallas as pl
from jax.experimental.pallas import tpu as pltpu
from jax.sharding import PartitionSpec as P

MESH = pl.DeviceIdType.MESH
F32, BF16 = jnp.float32, jnp.bfloat16
CORE = 128
PROBE = 256
HALF = 128
BAND = 104
ROWS = BAND + CORE + BAND
COLS = 3 * CORE
HALO = 100
REACH = 3
TVROWS = 136
UPROWS = 112
AMP_EPS = 0.1
LEARN_RATE = 0.2
TV_EPS = 1.0
TV_TAU = 0.1
TV_STEPS = 3


def tables():
    k, j = np.arange(HALF)[:, None], np.arange(HALF)[None, :]
    parts = []
    for odd in (0, 1):
        angle = 2.0 * np.pi * (((2 * k + odd) * j) % PROBE) / PROBE
        c, s = np.cos(angle) / math.sqrt(PROBE), np.sin(angle) / math.sqrt(PROBE)
        full = np.block([[c, s], [-s, c]])
        parts.append(full)
    out = []
    for full in (parts[0], parts[0].T, parts[1], parts[1].T):
        full = full.astype(np.float32)
        high = full.astype(BF16)
        out += [high, (full - high.astype(np.float32)).astype(BF16)]
    order = np.zeros((PROBE, PROBE), np.float32)
    order[np.arange(HALF), 2 * np.arange(HALF)] = 1
    order[HALF + np.arange(HALF), 2 * np.arange(HALF) + 1] = 1
    out += [order.astype(BF16), order.T.astype(BF16)]
    return np.stack(out)


def split(x):
    high = x.astype(BF16)
    return high, (x - high.astype(F32)).astype(BF16)


def mm(a, b):
    return jnp.dot(a, b, preferred_element_type=F32)


def left(tab, i, x):
    wh, wl = tab[2 * i], tab[2 * i + 1]
    xh, xl = split(x)
    return mm(wh, xh) + (mm(wh, xl) + mm(wl, xh))


def right(tab, i, x):
    wh, wl = tab[2 * i], tab[2 * i + 1]
    xh, xl = split(x)
    return mm(xh, wh) + (mm(xl, wh) + mm(xh, wl))


def cat(a, b, axis):
    return jnp.concatenate([a, b], axis=axis)


def forward(tab, re, im):
    h = HALF
    e = left(tab, 0, cat(re[:h] + re[h:], im[:h] + im[h:], 0))
    o = left(tab, 2, cat(re[:h] - re[h:], im[:h] - im[h:], 0))
    re, im = cat(e[:h], o[:h], 0), cat(e[h:], o[h:], 0)
    e = right(tab, 1, cat(re[:, :h] + re[:, h:], im[:, :h] + im[:, h:], 1))
    o = right(tab, 3, cat(re[:, :h] - re[:, h:], im[:, :h] - im[:, h:], 1))
    return cat(e[:, :h], o[:, :h], 1), cat(e[:, h:], o[:, h:], 1)


def inverse(tab, re, im):
    h = HALF
    e = left(tab, 1, cat(re[:h], im[:h], 0))
    o = left(tab, 3, cat(re[h:], im[h:], 0))
    s, d = e + o, e - o
    re, im = cat(s[:h], d[:h], 0), cat(s[h:], d[h:], 0)
    e = right(tab, 0, cat(re[:, :h], im[:, :h], 1))
    o = right(tab, 2, cat(re[:, h:], im[:, h:], 1))
    s, d = e + o, e - o
    return cat(s[:, :h], d[:, :h], 1), cat(s[:, h:], d[:, h:], 1)


def reorder(tab, x):
    for axis in (0, 1):
        total = None
        rest = x
        for _ in range(3):
            part = rest.astype(BF16)
            rest = rest - part.astype(F32)
            term = mm(tab[8], part) if axis == 0 else mm(part, tab[9])
            total = term if total is None else total + term
        x = total
    return x


class Place:
    def __init__(self):
        self.r, self.c = lax.axis_index("row"), lax.axis_index("col")
        nr, nc = lax.axis_size("row"), lax.axis_size("col")
        self.has = {"up": self.r > 0, "down": self.r < nr - 1, "left": self.c > 0, "right": self.c < nc - 1}
        self.to = {"up": {"row": self.r - 1}, "down": {"row": self.r + 1}, "left": {"col": self.c - 1}, "right": {"col": self.c + 1}}

    def barrier(self):
        sem = pltpu.get_barrier_semaphore()
        for side in OPPOSITE:
            @pl.when(self.has[side])
            def _():
                pl.semaphore_signal(sem, inc=1, device_id=self.to[side], device_id_type=MESH)
        pl.semaphore_wait(sem, sum(self.has[side].astype(jnp.int32) for side in OPPOSITE))


OPPOSITE = {"up": "down", "down": "up", "left": "right", "right": "left"}


class Copy:
    def __init__(self, place, side, src, dst, sems, i, also=None):
        self.op = pltpu.make_async_remote_copy(
            src_ref=src, dst_ref=dst, send_sem=sems[0].at[i], recv_sem=sems[1].at[i],
            device_id=place.to[side], device_id_type=MESH,
        )
        self.sends, self.gets = place.has[side], place.has[OPPOSITE[side]]
        if also is not None:
            self.sends, self.gets = self.sends & also, self.gets & also

    def start(self):
        pl.when(self.sends)(lambda: self.op.start())

    def got(self):
        pl.when(self.gets)(lambda: self.op.wait_recv())

    def sent(self):
        pl.when(self.sends)(lambda: self.op.wait_send())


def whole_kernel(
    pos, tr, w, probe_any, phase_any, amp_any, tab_any, out,
    probe, phase_ref, amp, tab, ext, wext, own, lband, from_left, from_right,
    total, pack, from_up, from_down, pack_up, pack_down, send, recv, local,
):
    place = Place()
    has = place.has
    sems = (send, recv)
    loads = []
    for n, (src, dst) in enumerate(((phase_any, phase_ref), (amp_any, amp), (tab_any, tab), (probe_any, probe))):
        load = pltpu.make_async_copy(src, dst, local.at[n])
        load.start()
        loads.append(load)
    place.barrier()
    mid = pl.ds(CORE, CORE)
    lanes = {"left": pl.ds(2 * CORE, CORE), "right": pl.ds(0, CORE)}
    jobs = [(BAND, tr.at[ch], ext.at[ch]) for ch in range(4)] + [(8, w, wext)]
    copies, corners = [], []
    for ch, (band, src, dst) in enumerate(jobs):
        base = 8 * ch
        top, low = pl.ds(0, band), pl.ds(band + CORE, band)
        group = [
            Copy(place, "up", src.at[pl.ds(0, band)], dst.at[low, mid], sems, base),
            Copy(place, "down", src.at[pl.ds(CORE - band, band)], dst.at[top, mid], sems, base + 1),
            Copy(place, "left", src, dst.at[pl.ds(band, CORE), lanes["left"]], sems, base + 2),
            Copy(place, "right", src, dst.at[pl.ds(band, CORE), lanes["right"]], sems, base + 3),
        ]
        for c in group:
            c.start()
        copies.append(group)
        corner = []
        for n, (rows, there) in enumerate(((low, has["down"]), (top, has["up"]))):
            for m, side in enumerate(("left", "right")):
                corner.append(Copy(place, side, dst.at[rows, mid], dst.at[rows, lanes[side]], sems, base + 4 + 2 * n + m, there))
        corners.append(corner)

    def forward_corners(channels):
        for ch in channels:
            for n in (0, 1):
                copies[ch][n].got()
                for m in (0, 1):
                    corners[ch][2 * n + m].start()

    def arrived(channels):
        for ch in channels:
            for c in copies[ch][2:] + corners[ch]:
                c.got()

    for (band, src, dst) in jobs:
        dst[band : band + CORE, CORE : 2 * CORE] = src[...]
        rows = dst.shape[0]

        @pl.when(jnp.logical_not(has["up"]))
        def _():
            dst[0:band, :] = jnp.zeros((band, COLS), F32)

        @pl.when(jnp.logical_not(has["down"]))
        def _():
            dst[band + CORE : rows, :] = jnp.zeros((band, COLS), F32)

        @pl.when(jnp.logical_not(has["left"]))
        def _():
            dst[:, 0:CORE] = jnp.zeros((rows, CORE), F32)

        @pl.when(jnp.logical_not(has["right"]))
        def _():
            dst[:, 2 * CORE :] = jnp.zeros((rows, CORE), F32)
    edges = (
        ("left", from_left), ("right", from_right), ("up", from_up), ("down", from_down),
        ("up", pack_up), ("down", pack_down),
    )
    for side, ref in edges:
        @pl.when(jnp.logical_not(has[side]))
        def _():
            ref[...] = jnp.zeros(ref.shape, F32)

    p, q = pos[0], pos[1]

    def window(ch):
        rows = pltpu.roll(ext[ch], ROWS - (BAND - HALO) - p, 0)[:PROBE]
        return pltpu.roll(rows, COLS - (q + (CORE - HALO)), 1)[:, :PROBE]

    across = {}

    def put(ch, grad):
        wide = cat(grad, jnp.zeros((PROBE, COLS - PROBE), F32), 1)
        at_own = lax.rem(q + (COLS - HALO + REACH), COLS)
        below = jnp.zeros((ROWS - PROBE, PROBE), F32)
        down_by = p + (BAND + REACH - HALO)
        own[ch] = pltpu.roll(cat(pltpu.roll(wide, at_own, 1)[:, :PROBE], below, 0), down_by, 0)
        turned = pltpu.roll(wide, q + (CORE - REACH - HALO), 1)[:, :CORE]
        lband[ch] = pltpu.roll(cat(turned, below[:, :CORE], 0), down_by, 0)
        across[ch] = (
            Copy(place, "right", own.at[ch, :, pl.ds(CORE, CORE)], from_left.at[ch], sems, 40 + 2 * ch),
            Copy(place, "left", lband.at[ch], from_right.at[ch], sems, 41 + 2 * ch),
        )
        for c in across[ch]:
            c.start()

    for load in loads[:3]:
        load.wait()
    phase = reorder(tab, phase_ref[...])
    kr, ki = jnp.cos(phase), jnp.sin(phase)
    measured = reorder(tab, amp[...])
    loads[3].wait()
    forward_corners((0, 1))
    arrived((0, 1))
    ar, ai = window(0), window(1)
    pr, pi = probe[0], probe[1]
    fr, fi = forward(tab, ar * pr - ai * pi, ar * pi + ai * pr)
    forward_corners((2, 3))
    wr, wi = inverse(tab, kr * fr - ki * fi, kr * fi + ki * fr)
    arrived((2, 3))
    forward_corners((4,))
    br, bi = window(2), window(3)
    fr, fi = forward(tab, br * wr - bi * wi, br * wi + bi * wr)
    factor = 1.0 - measured / jnp.sqrt(fr * fr + fi * fi + AMP_EPS)
    gr, gi = inverse(tab, fr * factor, fi * factor)
    put(2, wr * gr + wi * gi)
    put(3, wr * gi - wi * gr)
    along = []
    lane = lax.broadcasted_iota(jnp.int32, (ROWS, CORE), 1)

    def fold(ch):
        for c in across[ch]:
            c.got()
        shifted = pltpu.roll(from_right[ch], 2 * REACH, 1)
        total[ch] = own[ch, :, :CORE] + from_left[ch] + jnp.where(lane >= 2 * REACH, shifted, 0.0)
        rest = jnp.where(lane < 2 * REACH, own[ch, :, CORE:] + shifted, 0.0)
        pair = (
            Copy(place, "down", total.at[ch, pl.ds(ROWS - BAND, BAND)], from_up.at[ch], sems, 48 + 2 * ch),
            Copy(place, "up", total.at[ch, pl.ds(0, UPROWS)], from_down.at[ch], sems, 49 + 2 * ch),
        )
        for c in pair:
            c.start()
        along.append(pair)
        return pltpu.roll(rest, 8 * ch, 1) if ch else rest

    fr, fi = forward(tab, br * gr + bi * gi, br * gi - bi * gr)
    gr, gi = inverse(tab, kr * fr + ki * fi, kr * fi - ki * fr)
    put(0, pr * gr + pi * gi)
    put(1, pr * gi - pi * gr)
    packed = fold(2) + fold(3) + fold(0) + fold(1)

    def compact(rows):
        rows = cat(rows, jnp.zeros((CORE - rows.shape[0], CORE), F32), 0)
        parts = [rows[32 * k : 32 * k + 32] for k in range(4)]
        return parts[0] + sum(pltpu.roll(parts[k], 32 * k, 1) for k in (1, 2, 3))

    def spread_out(x):
        return jnp.concatenate([x] + [pltpu.roll(x, CORE - 32 * k, 1) for k in (1, 2, 3)], axis=0)

    pack[0] = compact(packed[ROWS - BAND :])
    pack[1] = compact(packed[:UPROWS])
    pair = (
        Copy(place, "down", pack.at[0], pack_up, sems, 56),
        Copy(place, "up", pack.at[1], pack_down, sems, 57),
    )
    for c in pair:
        c.start()
    along.append(pair)

    arrived((4,))
    shape = (TVROWS, PROBE)
    row_at = lax.broadcasted_iota(jnp.int32, shape, 0) - REACH + place.r * CORE
    col_at = lax.broadcasted_iota(jnp.int32, shape, 1) - REACH + place.c * CORE
    inside = (row_at >= 0) & (row_at < lax.axis_size("row") * CORE) & (col_at >= 0) & (col_at < lax.axis_size("col") * CORE)
    inside = inside.astype(F32)

    def cut(ref_rows):
        return pltpu.roll(ref_rows, COLS - (CORE - REACH), 1)[:, :PROBE]

    weight = cut(wext[8 - REACH : 8 - REACH + TVROWS, :]) * inside
    for pair in along:
        for c in pair:
            c.got()

    def joined(mine, upper, lower):
        upper = cat(upper, jnp.zeros((TVROWS - BAND, CORE), F32), 0)
        lower = cat(jnp.zeros((TVROWS - UPROWS, CORE), F32), lower, 0)
        return mine[BAND : BAND + TVROWS] + upper + lower

    side = joined(packed, spread_out(pack_up[...])[:BAND], spread_out(pack_down[...])[:UPROWS])
    fields = []
    for ch in range(4):
        grad = joined(total[ch], from_up[ch], from_down[ch])
        rest = pltpu.roll(side, CORE - 8 * ch, 1) if ch else side
        field = cut(ext[ch, BAND - REACH : BAND - REACH + TVROWS, :])
        fields.append((field - LEARN_RATE * cat(grad, rest, 1)) * inside)
    for s in range(2):
        pair = fields[2 * s : 2 * s + 2]
        for _ in range(TV_STEPS):
            down = [pltpu.roll(f, TVROWS - 1, 0) - f for f in pair]
            along_row = [pltpu.roll(f, PROBE - 1, 1) - f for f in pair]
            square = down[0] * down[0] + along_row[0] * along_row[0] + (down[1] * down[1] + along_row[1] * along_row[1])
            gain = weight / jnp.sqrt(square + TV_EPS)
            fresh = []
            for f, d, r in zip(pair, down, along_row):
                d, r = gain * d, gain * r
                update = d - pltpu.roll(d, 1, 0) + (r - pltpu.roll(r, 1, 1))
                fresh.append((f + TV_TAU * update) * inside)
            pair = fresh
        for c in range(2):
            out[2 * s + c] = pltpu.roll(pair[c], PROBE - REACH, 1)[REACH : REACH + CORE, :CORE]
    for group in copies + corners + [across[ch] for ch in range(4)] + along:
        for c in group:
            c.sent()


def body(transmission, probe, fresnel_phase, amplitudes, positions, tv_weight):
    vmem, anywhere = (pl.BlockSpec(memory_space=m) for m in (pltpu.VMEM, pl.ANY))
    tab = tables()
    out = pl.pallas_call(
        whole_kernel,
        out_shape=jax.ShapeDtypeStruct((4, CORE, CORE), F32),
        in_specs=[pl.BlockSpec(memory_space=pltpu.SMEM), vmem, vmem] + [anywhere] * 4,
        out_specs=vmem,
        scratch_shapes=[
            pltpu.VMEM((2, PROBE, PROBE), F32),
            pltpu.VMEM((PROBE, PROBE), F32),
            pltpu.VMEM((PROBE, PROBE), F32),
            pltpu.VMEM(tab.shape, BF16),
            pltpu.VMEM((4, ROWS, COLS), F32),
            pltpu.VMEM((CORE + 16, COLS), F32),
            pltpu.VMEM((4, ROWS, PROBE), F32),
            pltpu.VMEM((4, ROWS, CORE), F32),
            pltpu.VMEM((4, ROWS, CORE), F32),
            pltpu.VMEM((4, ROWS, CORE), F32),
            pltpu.VMEM((4, ROWS, CORE), F32),
            pltpu.VMEM((2, 32, CORE), F32),
            pltpu.VMEM((4, BAND, CORE), F32),
            pltpu.VMEM((4, UPROWS, CORE), F32),
            pltpu.VMEM((32, CORE), F32),
            pltpu.VMEM((32, CORE), F32),
            pltpu.SemaphoreType.DMA((58,)),
            pltpu.SemaphoreType.DMA((58,)),
            pltpu.SemaphoreType.DMA((4,)),
        ],
        compiler_params=pltpu.CompilerParams(collective_id=0, has_side_effects=True),
        name="ptycho",
    )(
        positions.reshape(2), transmission.reshape(4, CORE, CORE), tv_weight, probe, fresnel_phase,
        amplitudes.reshape(PROBE, PROBE), jnp.asarray(tab),
    )
    return out.reshape(2, 2, CORE, CORE)


def solution(mesh):
    placed = (
        P(None, None, "row", "col"),
        P(),
        P(),
        P("row", "col", None, None, None),
        P("row", "col", None, None),
        P("row", "col"),
    )
    return jax.shard_map(
        body, mesh=mesh, in_specs=placed, out_specs=P(None, None, "row", "col"), check_vma=False
    )
```

```python
import functools
import math

import jax
import jax.numpy as jnp
import numpy as np
from jax import lax
from jax.experimental import pallas as pl
from jax.experimental.pallas import tpu as pltpu
from jax.sharding import PartitionSpec as P

MESH = pl.DeviceIdType.MESH
F32, BF16 = jnp.float32, jnp.bfloat16
CORE = 128
PROBE = 256
HALF = 128
BAND = 104
ROWS = BAND + CORE + BAND
COLS = 3 * CORE
HALO = 100
REACH = 3
TVROWS = 136
UPROWS = 112
AMP_EPS = 0.1
LEARN_RATE = 0.2
TV_EPS = 1.0
TV_TAU = 0.1
TV_STEPS = 3


def tables():
    k, j = np.arange(HALF)[:, None], np.arange(HALF)[None, :]
    parts = []
    for odd in (0, 1):
        angle = 2.0 * np.pi * (((2 * k + odd) * j) % PROBE) / PROBE
        c, s = np.cos(angle) / math.sqrt(PROBE), np.sin(angle) / math.sqrt(PROBE)
        full = np.block([[c, s], [-s, c]])
        parts.append(full)
    out = []
    for full in (parts[0], parts[0].T, parts[1], parts[1].T):
        full = full.astype(np.float32)
        high = full.astype(BF16)
        out += [high, (full - high.astype(np.float32)).astype(BF16)]
    order = np.zeros((PROBE, PROBE), np.float32)
    order[np.arange(HALF), 2 * np.arange(HALF)] = 1
    order[HALF + np.arange(HALF), 2 * np.arange(HALF) + 1] = 1
    out += [order.astype(BF16), order.T.astype(BF16)]
    return np.stack(out)


def split(x):
    high = x.astype(BF16)
    return high, (x - high.astype(F32)).astype(BF16)


def mm(a, b):
    return jnp.dot(a, b, preferred_element_type=F32)


def left(tab, i, x):
    wh, wl = tab[2 * i], tab[2 * i + 1]
    xh, xl = split(x)
    return mm(wh, xh) + (mm(wh, xl) + mm(wl, xh))


def right(tab, i, x):
    wh, wl = tab[2 * i], tab[2 * i + 1]
    xh, xl = split(x)
    return mm(xh, wh) + (mm(xl, wh) + mm(xh, wl))


def cat(a, b, axis):
    return jnp.concatenate([a, b], axis=axis)


def forward(tab, re, im):
    h = HALF
    e = left(tab, 0, cat(re[:h] + re[h:], im[:h] + im[h:], 0))
    o = left(tab, 2, cat(re[:h] - re[h:], im[:h] - im[h:], 0))
    re, im = cat(e[:h], o[:h], 0), cat(e[h:], o[h:], 0)
    e = right(tab, 1, cat(re[:, :h] + re[:, h:], im[:, :h] + im[:, h:], 1))
    o = right(tab, 3, cat(re[:, :h] - re[:, h:], im[:, :h] - im[:, h:], 1))
    return cat(e[:, :h], o[:, :h], 1), cat(e[:, h:], o[:, h:], 1)


def inverse(tab, re, im):
    h = HALF
    e = left(tab, 1, cat(re[:h], im[:h], 0))
    o = left(tab, 3, cat(re[h:], im[h:], 0))
    s, d = e + o, e - o
    re, im = cat(s[:h], d[:h], 0), cat(s[h:], d[h:], 0)
    e = right(tab, 0, cat(re[:, :h], im[:, :h], 1))
    o = right(tab, 2, cat(re[:, h:], im[:, h:], 1))
    s, d = e + o, e - o
    return cat(s[:, :h], d[:, :h], 1), cat(s[:, h:], d[:, h:], 1)


def reorder(tab, x):
    for axis in (0, 1):
        total = None
        rest = x
        for _ in range(3):
            part = rest.astype(BF16)
            rest = rest - part.astype(F32)
            term = mm(tab[8], part) if axis == 0 else mm(part, tab[9])
            total = term if total is None else total + term
        x = total
    return x


class Place:
    def __init__(self):
        self.r, self.c = lax.axis_index("row"), lax.axis_index("col")
        nr, nc = lax.axis_size("row"), lax.axis_size("col")
        self.has = {"up": self.r > 0, "down": self.r < nr - 1, "left": self.c > 0, "right": self.c < nc - 1}
        self.relay = nr % 2 == 0
        self.has["up2"], self.has["down2"] = self.r > 1, self.r < nr - 2
        odd = lax.rem(self.r, 2) == 1
        self.odd, self.even = odd, jnp.logical_not(odd)
        self.to = {"up": {"row": self.r - 1}, "down": {"row": self.r + 1}, "left": {"col": self.c - 1}, "right": {"col": self.c + 1}}

    def barrier(self):
        self.to["up2"], self.to["down2"] = {"row": self.r - 2}, {"row": self.r + 2}
        sem = pltpu.get_barrier_semaphore()
        for side in OPPOSITE:
            @pl.when(self.has[side])
            def _():
                pl.semaphore_signal(sem, inc=1, device_id=self.to[side], device_id_type=MESH)
        pl.semaphore_wait(sem, sum(self.has[side].astype(jnp.int32) for side in OPPOSITE))


OPPOSITE = {"up": "down", "down": "up", "left": "right", "right": "left", "up2": "down2", "down2": "up2"}


class Copy:
    def __init__(self, place, side, src, dst, sems, i, also=None, gets=None):
        self.op = pltpu.make_async_remote_copy(
            src_ref=src, dst_ref=dst, send_sem=sems[0].at[i], recv_sem=sems[1].at[i],
            device_id=place.to[side], device_id_type=MESH,
        )
        self.sends, self.gets = place.has[side], place.has[OPPOSITE[side]]
        if also is not None:
            self.sends, self.gets = self.sends & also, self.gets & (also if gets is None else gets)

    def start(self):
        pl.when(self.sends)(lambda: self.op.start())

    def got(self):
        pl.when(self.gets)(lambda: self.op.wait_recv())

    def sent(self):
        pl.when(self.sends)(lambda: self.op.wait_send())


def whole_kernel(
    pos, tr, w, probe_any, phase_any, amp_any, tab_any, out, last,
    probe, phase_ref, amp, tab, ext, wext, own, lband, from_left, from_right,
    total, pack, from_up, from_down, pack_up, pack_down, send, recv, local,
):
    place = Place()
    has = place.has
    sems = (send, recv)
    loads = []
    for n, (src, dst) in enumerate(((phase_any, phase_ref), (amp_any, amp), (tab_any, tab), (probe_any, probe))):
        load = pltpu.make_async_copy(src, dst, local.at[n])
        load.start()
        loads.append(load)
    place.barrier()
    mid = pl.ds(CORE, CORE)
    lanes = {"left": pl.ds(2 * CORE, CORE), "right": pl.ds(0, CORE)}
    jobs = [(BAND, tr.at[ch], ext.at[ch]) for ch in range(4)] + [(8, w, wext)]
    copies, corners, parts, relays = [], [], [], []
    odd, even = place.odd, place.even
    odd_to_even, even_to_odd = ((odd, even), (even, odd)) if place.relay else ((), ())
    own_rows = CORE - BAND
    common = BAND - own_rows
    for ch, (band, src, dst) in enumerate(jobs):
        base = 8 * ch
        top, low = pl.ds(0, band), pl.ds(band + CORE, band)
        group = [
            Copy(place, "up", src.at[pl.ds(0, band)], dst.at[low, mid], sems, base, *(odd_to_even if ch < 4 else ())),
            Copy(place, "down", src.at[pl.ds(CORE - band, band)], dst.at[top, mid], sems, base + 1, *(even_to_odd if ch < 4 else ())),
            Copy(place, "left", src, dst.at[pl.ds(band, CORE), lanes["left"]], sems, base + 2),
            Copy(place, "right", src, dst.at[pl.ds(band, CORE), lanes["right"]], sems, base + 3),
        ]
        for c in group:
            c.start()
        copies.append(group)
        if ch < 4 and place.relay:
            part = [
                Copy(place, "up", src.at[pl.ds(0, own_rows)], dst.at[pl.ds(BAND + CORE, own_rows), mid], sems, 60 + 4 * ch, even, odd),
                Copy(place, "down", src.at[pl.ds(BAND, own_rows)], dst.at[pl.ds(common, own_rows), mid], sems, 61 + 4 * ch, odd, even),
            ]
            for c in part:
                c.start()
            parts.append(part)
            held_top, held_low = pl.ds(0, common), pl.ds(BAND + CORE + own_rows, common)
            relays.append([
                Copy(place, "up2", dst.at[held_top, mid], dst.at[held_low, mid], sems, 62 + 4 * ch, odd),
                Copy(place, "down2", dst.at[held_low, mid], dst.at[held_top, mid], sems, 63 + 4 * ch, even),
            ])
        corner = []
        for n, (rows, there) in enumerate(((low, has["down"]), (top, has["up"]))):
            for m, side in enumerate(("left", "right")):
                corner.append(Copy(place, side, dst.at[rows, mid], dst.at[rows, lanes[side]], sems, base + 4 + 2 * n + m, there))
        corners.append(corner)

    def forward_bands(channels):
        for ch in channels:
            for c in copies[ch][:2]:
                c.got()
            if ch < 4 and place.relay:
                for c in relays[ch]:
                    c.start()

    def forward_corners(channels):
        for ch in channels:
            if ch < 4 and place.relay:
                for c in parts[ch] + relays[ch]:
                    c.got()
            for n in (0, 1):
                for m in (0, 1):
                    corners[ch][2 * n + m].start()

    def arrived(channels):
        for ch in channels:
            for c in copies[ch][2:] + corners[ch]:
                c.got()

    for (band, src, dst) in jobs:
        dst[band : band + CORE, CORE : 2 * CORE] = src[...]
        rows = dst.shape[0]

        @pl.when(jnp.logical_not(has["up"]))
        def _():
            dst[0:band, :] = jnp.zeros((band, COLS), F32)

        @pl.when(jnp.logical_not(has["down"]))
        def _():
            dst[band + CORE : rows, :] = jnp.zeros((band, COLS), F32)

        @pl.when(jnp.logical_not(has["left"]))
        def _():
            dst[:, 0:CORE] = jnp.zeros((rows, CORE), F32)

        @pl.when(jnp.logical_not(has["right"]))
        def _():
            dst[:, 2 * CORE :] = jnp.zeros((rows, CORE), F32)
    edges = (
        ("left", from_left), ("right", from_right), ("up", from_up), ("down", from_down),
        ("up", pack_up), ("down", pack_down),
    )
    for side, ref in edges:
        @pl.when(jnp.logical_not(has[side]))
        def _():
            ref[...] = jnp.zeros(ref.shape, F32)

    p, q = pos[0], pos[1]

    def window(ch):
        rows = pltpu.roll(ext[ch], ROWS - (BAND - HALO) - p, 0)[:PROBE]
        return pltpu.roll(rows, COLS - (q + (CORE - HALO)), 1)[:, :PROBE]

    across = {}

    def put(ch, grad):
        wide = cat(grad, jnp.zeros((PROBE, COLS - PROBE), F32), 1)
        at_own = lax.rem(q + (COLS - HALO + REACH), COLS)
        below = jnp.zeros((ROWS - PROBE, PROBE), F32)
        down_by = p + (BAND + REACH - HALO)
        own[ch] = pltpu.roll(cat(pltpu.roll(wide, at_own, 1)[:, :PROBE], below, 0), down_by, 0)
        turned = pltpu.roll(wide, q + (CORE - REACH - HALO), 1)[:, :CORE]
        lband[ch] = pltpu.roll(cat(turned, below[:, :CORE], 0), down_by, 0)
        across[ch] = (
            Copy(place, "right", own.at[ch, :, pl.ds(CORE, CORE)], from_left.at[ch], sems, 40 + 2 * ch),
            Copy(place, "left", lband.at[ch], from_right.at[ch], sems, 41 + 2 * ch),
        )
        for c in across[ch]:
            c.start()

    for load in loads[:3]:
        load.wait()
    phase = reorder(tab, phase_ref[...])
    kr, ki = jnp.cos(phase), jnp.sin(phase)
    measured = reorder(tab, amp[...])
    loads[3].wait()
    forward_bands((0, 1))
    forward_corners((0, 1))
    forward_bands((2, 3))
    arrived((0, 1))
    ar, ai = window(0), window(1)
    pr, pi = probe[0], probe[1]
    fr, fi = forward(tab, ar * pr - ai * pi, ar * pi + ai * pr)
    forward_corners((2, 3))
    wr, wi = inverse(tab, kr * fr - ki * fi, kr * fi + ki * fr)
    arrived((2, 3))
    forward_bands((4,))
    forward_corners((4,))
    br, bi = window(2), window(3)
    fr, fi = forward(tab, br * wr - bi * wi, br * wi + bi * wr)
    factor = 1.0 - measured / jnp.sqrt(fr * fr + fi * fi + AMP_EPS)
    gr, gi = inverse(tab, fr * factor, fi * factor)
    put(2, wr * gr + wi * gi)
    put(3, wr * gi - wi * gr)
    along = []
    lane = lax.broadcasted_iota(jnp.int32, (ROWS, CORE), 1)

    def fold(ch):
        for c in across[ch]:
            c.got()
        shifted = pltpu.roll(from_right[ch], 2 * REACH, 1)
        total[ch] = own[ch, :, :CORE] + from_left[ch] + jnp.where(lane >= 2 * REACH, shifted, 0.0)
        rest = jnp.where(lane < 2 * REACH, own[ch, :, CORE:] + shifted, 0.0)
        pair = (
            Copy(place, "down", total.at[ch, pl.ds(ROWS - BAND, BAND)], from_up.at[ch], sems, 48 + 2 * ch),
            Copy(place, "up", total.at[ch, pl.ds(0, UPROWS)], from_down.at[ch], sems, 49 + 2 * ch),
        )
        for c in pair:
            c.start()
        along.append(pair)
        return pltpu.roll(rest, 8, 1) if ch % 2 else rest

    fr, fi = forward(tab, br * gr + bi * gi, br * gi - bi * gr)
    gr, gi = inverse(tab, kr * fr + ki * fi, kr * fi - ki * fr)
    border = {2: fold(2)}
    put(0, pr * gr + pi * gi)
    put(1, pr * gi - pi * gr)

    def compact(rows):
        rows = cat(rows, jnp.zeros((CORE - rows.shape[0], CORE), F32), 0)
        return rows[:16] + sum(pltpu.roll(rows[16 * k : 16 * k + 16], 16 * k, 1) for k in range(1, 8))

    def spread_out(x):
        return jnp.concatenate([x] + [pltpu.roll(x, CORE - 16 * k, 1) for k in range(1, 8)], axis=0)

    def send_border(sl):
        packed = border[2 * sl] + border[2 * sl + 1]
        pack[sl, 0] = compact(packed[ROWS - BAND :])
        pack[sl, 1] = compact(packed[:UPROWS])
        pair = (
            Copy(place, "down", pack.at[sl, 0], pack_up.at[sl], sems, 56 + 2 * sl),
            Copy(place, "up", pack.at[sl, 1], pack_down.at[sl], sems, 57 + 2 * sl),
        )
        for c in pair:
            c.start()
        along.append(pair)
        return packed

    border[3] = fold(3)
    packed = {1: send_border(1)}
    border[0] = fold(0)
    border[1] = fold(1)
    packed[0] = send_border(0)

    arrived((4,))
    shape = (TVROWS, PROBE)
    row_at = lax.broadcasted_iota(jnp.int32, shape, 0) - REACH + place.r * CORE
    col_at = lax.broadcasted_iota(jnp.int32, shape, 1) - REACH + place.c * CORE
    inside = (row_at >= 0) & (row_at < lax.axis_size("row") * CORE) & (col_at >= 0) & (col_at < lax.axis_size("col") * CORE)
    inside = inside.astype(F32)

    def cut(ref_rows):
        return pltpu.roll(ref_rows, COLS - (CORE - REACH), 1)[:, :PROBE]

    def joined(mine, upper, lower):
        upper = cat(upper, jnp.zeros((TVROWS - BAND, CORE), F32), 0)
        lower = cat(jnp.zeros((TVROWS - UPROWS, CORE), F32), lower, 0)
        return mine[BAND : BAND + TVROWS] + upper + lower

    weight = cut(wext[8 - REACH : 8 - REACH + TVROWS, :]) * inside
    for sl, arrivals in ((1, along[:3]), (0, along[3:])):
        for pair in arrivals:
            for c in pair:
                c.got()
        side = joined(packed[sl], spread_out(pack_up[sl])[:BAND], spread_out(pack_down[sl])[:UPROWS])
        pair = []
        for c in range(2):
            ch = 2 * sl + c
            grad = joined(total[ch], from_up[ch], from_down[ch])
            rest = pltpu.roll(side, CORE - 8, 1) if c else side
            field = cut(ext[ch, BAND - REACH : BAND - REACH + TVROWS, :])
            pair.append((field - LEARN_RATE * cat(grad, rest, 1)) * inside)
        for step in range(TV_STEPS):
            down = [pltpu.roll(f, TVROWS - 1, 0) - f for f in pair]
            along_row = [pltpu.roll(f, PROBE - 1, 1) - f for f in pair]
            square = down[0] * down[0] + along_row[0] * along_row[0] + (down[1] * down[1] + along_row[1] * along_row[1])
            gain = weight / jnp.sqrt(square + TV_EPS)
            fresh = []
            for c, (f, d, r) in enumerate(zip(pair, down, along_row)):
                d, r = gain * d, gain * r
                update = d - pltpu.roll(d, 1, 0) + (r - pltpu.roll(r, 1, 1))
                if step < TV_STEPS - 1:
                    fresh.append((f + TV_TAU * update) * inside)
                else:
                    for ref, value in ((out, f), (last, update)):
                        ref[2 * sl + c] = pltpu.roll(value, PROBE - REACH, 1)[REACH : REACH + CORE, :CORE]
            pair = fresh
    for group in copies + corners + parts + relays + [across[ch] for ch in range(4)] + along:
        for c in group:
            c.sent()


def body(transmission, probe, fresnel_phase, amplitudes, positions, tv_weight):
    vmem, anywhere = (pl.BlockSpec(memory_space=m) for m in (pltpu.VMEM, pl.ANY))
    tab = tables()
    field, update = pl.pallas_call(
        whole_kernel,
        out_shape=(jax.ShapeDtypeStruct((4, CORE, CORE), F32),) * 2,
        in_specs=[pl.BlockSpec(memory_space=pltpu.SMEM), vmem, vmem] + [anywhere] * 4,
        out_specs=(vmem, vmem),
        scratch_shapes=[
            pltpu.VMEM((2, PROBE, PROBE), F32),
            pltpu.VMEM((PROBE, PROBE), F32),
            pltpu.VMEM((PROBE, PROBE), F32),
            pltpu.VMEM(tab.shape, BF16),
            pltpu.VMEM((4, ROWS, COLS), F32),
            pltpu.VMEM((CORE + 16, COLS), F32),
            pltpu.VMEM((4, ROWS, PROBE), F32),
            pltpu.VMEM((4, ROWS, CORE), F32),
            pltpu.VMEM((4, ROWS, CORE), F32),
            pltpu.VMEM((4, ROWS, CORE), F32),
            pltpu.VMEM((4, ROWS, CORE), F32),
            pltpu.VMEM((2, 2, 16, CORE), F32),
            pltpu.VMEM((4, BAND, CORE), F32),
            pltpu.VMEM((4, UPROWS, CORE), F32),
            pltpu.VMEM((2, 16, CORE), F32),
            pltpu.VMEM((2, 16, CORE), F32),
            pltpu.SemaphoreType.DMA((76,)),
            pltpu.SemaphoreType.DMA((76,)),
            pltpu.SemaphoreType.DMA((4,)),
        ],
        compiler_params=pltpu.CompilerParams(collective_id=0, has_side_effects=True),
        name="ptycho",
    )(
        positions.reshape(2), transmission.reshape(4, CORE, CORE), tv_weight, probe, fresnel_phase,
        amplitudes.reshape(PROBE, PROBE), jnp.asarray(tab),
    )
    return (field + TV_TAU * update).reshape(2, 2, CORE, CORE)


def solution(mesh):
    placed = (
        P(None, None, "row", "col"),
        P(),
        P(),
        P("row", "col", None, None, None),
        P("row", "col", None, None),
        P("row", "col"),
    )
    return jax.shard_map(
        body, mesh=mesh, in_specs=placed, out_specs=P(None, None, "row", "col"), check_vma=False
    )
```
